32 devices in a mesh: light: 4 (over z), view: 8 (over y, x, core).
Axes of the slice: x: 2, y: 2, z: 4, core: 2. Of those that a mesh axis runs over, the one named last changes fastest.
Arguments:
- density: float32 [8, 128, 1024], P('light', 'view'), may hold values from 0 to 1
- colour: bfloat16 [3, 8, 128, 1024], P(None, 'light', 'view'), may hold values from 0 to 1
- absorb: float32 [3], replicated, may hold values from 0.3 to 3
- light_in: float32 [3, 128, 1024], P(None, 'view'), may hold values from 0.5 to 1.5
Outputs:
- image: float32 [4, 8, 1024], P(None, 'light', 'view')
The draws below stay inside these ranges and needn't reach their ends.
All inputs are finite; a program needn't handle non-finite values.
Results may differ from the reference program's by a relative error of at most 0.0003.
Values sent between devices are 32-bit elements; how exact they have to be, the bound alone decides.
A program may use at most 64 MiB of HBM per device.

```python
import math
import jax
import jax.numpy as jnp
from jax import lax

X = 1024
NZ = 8
NY = 128


def shard_levels(key, dims, split, least, largest):
    def one(position, parts):
        heights = jax.random.uniform(jax.random.fold_in(jax.random.fold_in(key, 6), position), (parts,), jnp.float32, least / len(split), largest / len(split))
        return jnp.repeat(jnp.exp(heights), dims[position] // parts).reshape((-1,) + (1,) * (len(dims) - position - 1))

    gain = one(*split[0])
    for cut in split[1:]:
        gain = gain * one(*cut)
    return gain


def setup_inputs(seed: int = 0) -> dict:
    arg_keys = jax.random.split(jax.random.key(seed), 5)
    return {
        "density": jnp.clip(1.0 * jax.random.uniform(arg_keys[0], (NZ, NY, X), jnp.float32) ** shard_levels(arg_keys[0], (NZ, NY, X), ((0, 4), (1, 8)), -0.2, 0.2), 0.0, 1.0),
        "colour": jnp.clip(1.0 * jax.random.uniform(arg_keys[1], (3, NZ, NY, X), jnp.float32) ** shard_levels(arg_keys[1], (3, NZ, NY, X), ((1, 4), (2, 8)), -0.2, 0.2), 0.0, 1.0).astype(jnp.bfloat16),
        "absorb": jnp.clip(jnp.exp(jax.random.uniform(arg_keys[2], (3,), jnp.float32, math.log(0.3), math.log(3.0))), 0.3, 3.0),
        "light_in": jnp.clip(0.5 + 1.0 * jax.random.uniform(arg_keys[3], (3, NY, X), jnp.float32) ** shard_levels(arg_keys[3], (3, NY, X), ((1, 8),), -0.2, 0.2), 0.5, 1.5),
    }


view_scale = 0.25
blur_center = 0.5
blur_edge = 0.1
blur_corner = 0.025


def opacity_of(values):
    return 0.01 * values + 0.03 * values * values * values


def blur_inner(widened):
    height = widened.shape[1] - 2
    width = widened.shape[2]
    padded = jnp.pad(widened, ((0, 0), (0, 0), (1, 1)))

    def part(down, across):
        return padded[:, 1 + down:1 + down + height, 1 + across:1 + across + width]

    edges = part(-1, 0) + part(1, 0) + part(0, -1) + part(0, 1)
    corners = part(-1, -1) + part(-1, 1) + part(1, -1) + part(1, 1)
    return blur_center * part(0, 0) + blur_edge * edges + blur_corner * corners


def reference(density, colour, absorb, light_in):
    decay = absorb[:, None, None]

    def slice_step(light, slab):
        slab_density, tint = slab
        opacity = opacity_of(slab_density)
        alpha = view_scale * opacity
        emitted = alpha[None] * tint.astype(jnp.float32) * light
        transmit = jnp.cumprod(1.0 - alpha, axis=0)
        before = jnp.concatenate([jnp.ones_like(transmit[:1]), transmit[:-1]], axis=0)
        colour_sum = jnp.sum(before[None] * emitted, axis=1)
        image_row = jnp.concatenate([colour_sum, (1.0 - transmit[-1])[None]], axis=0)
        dimmed = light * (1.0 - decay * opacity[None])
        passed_on = blur_inner(jnp.pad(dimmed, ((0, 0), (1, 1), (0, 0))))
        return passed_on, image_row

    tints = jnp.moveaxis(colour, 1, 0)
    unused, image_rows = lax.scan(slice_step, light_in, (density, tints))
    return jnp.moveaxis(image_rows, 0, 1)
```

```python
import functools

import jax
import jax.numpy as jnp
from jax import lax
from jax.experimental import pallas as pl
from jax.experimental.pallas import tpu as pltpu
from jax.sharding import PartitionSpec as P

view_scale = 0.25
blur_center = 0.5
blur_edge = 0.1
blur_corner = 0.025

MESH = pl.DeviceIdType.MESH


def opacity_of(values):
    return 0.01 * values + 0.03 * values * values * values


def kernel(
    lights,
    views,
    density_hbm,
    colour_hbm,
    absorb_ref,
    light_hbm,
    out_ref,
    density_ref,
    colour_ref,
    light_ref,
    load_sem,
    first,
    first_top,
    first_bottom,
    first_above,
    first_below,
    first_opacity,
    first_send,
    first_recv,
    seed_above,
    seed_below,
    seed_recv,
    plane_ref,
    wide_top,
    wide_bottom,
    wide_send,
    wide_recv,
    own,
    above,
    below,
    passed,
    edge_top,
    edge_bottom,
    seed_top,
    seed_bottom,
    dens_top,
    dens_bottom,
    dens_above,
    dens_below,
    ring_opacity,
    weight,
    rows_a,
    rows_b,
    send_a,
    send_b,
    got_a,
    got_b,
    own_send,
    own_recv,
    edge_send,
    edge_recv,
    seed_send,
    dens_send,
    dens_recv,
    a_send,
    a_recv,
    b_send,
    b_recv,
):
    l = lax.axis_index("light")
    v = lax.axis_index("view")
    slices, height, width = density_ref.shape
    channels = light_ref.shape[0]
    spare = plane_ref.shape[0] - height
    reach2 = seed_above.shape[1]
    cols = out_ref.shape[1]
    has_above = v > 0
    has_below = v < views - 1
    has_next = l < lights - 1
    is_first = l == 0
    even = lax.rem(l, 2) == 0
    odd = lax.rem(l, 2) == 1
    gives = (is_first | odd) & has_next
    takes = (l == 1) | (even & (l > 1))
    jumps = even & (l < lights - 2)
    steps = even & (l > 1) & has_next

    barrier = pltpu.get_barrier_semaphore()

    def greet(dl, dv):
        pl.semaphore_signal(
            barrier, inc=1, device_id={"light": l + dl, "view": v + dv}, device_id_type=MESH
        )

    for step in range(1, views):
        pl.semaphore_signal(
            barrier,
            inc=1,
            device_id={"light": l, "view": lax.rem(v + step, views)},
            device_id_type=MESH,
        )
    for dl in (-2, -1, 1, 2):
        l_ok = l >= -dl if dl < 0 else l < lights - dl
        if abs(dl) == 2:
            l_ok = l_ok & even

        @pl.when(l_ok)
        def _():
            greet(dl, 0)

        for dv in (-1, 1):

            @pl.when(l_ok & (has_above if dv < 0 else has_below))
            def _():
                greet(dl, dv)

    one = jnp.int32(1)
    zero = jnp.int32(0)
    lines = jnp.where(l > 0, one, zero) + jnp.where(has_next, one, zero)
    lines = lines + jnp.where(even & (l > 1), one, zero) + jnp.where(jumps, one, zero)
    sides = one + jnp.where(has_above, one, zero) + jnp.where(has_below, one, zero)

    loads = [
        pltpu.make_async_copy(src, dst, load_sem.at[i])
        for i, (src, dst) in enumerate(
            ((density_hbm, density_ref), (light_hbm, light_ref), (colour_hbm, colour_ref))
        )
    ]
    for load in loads:
        load.start()

    @pl.when(jnp.logical_not(has_above))
    def _():
        above[...] = jnp.zeros_like(above)
        dens_above[...] = jnp.zeros_like(dens_above)
        first_above[...] = jnp.zeros_like(first_above)
        seed_above[...] = jnp.zeros_like(seed_above)

    @pl.when(jnp.logical_not(has_below))
    def _():
        below[...] = jnp.zeros_like(below)
        dens_below[...] = jnp.zeros_like(dens_below)
        first_below[...] = jnp.zeros_like(first_below)
        seed_below[...] = jnp.zeros_like(seed_below)

    loads[0].wait()
    dens_top[...] = density_ref[:, :slices, :]
    dens_bottom[...] = density_ref[:, height - slices :, :]

    @pl.when(gives)
    def _():
        first_top[...] = density_ref[:, :reach2, :]
        first_bottom[...] = density_ref[:, height - reach2 :, :]

    loads[1].wait()

    @pl.when(l <= 1)
    def _():
        seed_top[...] = light_ref[:, :reach2, :]
        seed_bottom[...] = light_ref[:, height - reach2 :, :]

    pl.semaphore_wait(barrier, views - 1 + lines * sides)

    def copy(src, dst, send, recv, to_l, to_v):
        return pltpu.make_async_remote_copy(
            src_ref=src,
            dst_ref=dst,
            send_sem=send,
            recv_sem=recv,
            device_id={"light": to_l, "view": to_v},
            device_id_type=MESH,
        )

    def dens_up():
        return copy(dens_top, dens_below, dens_send.at[0], dens_recv.at[0], l, v - 1)

    def dens_down():
        return copy(dens_bottom, dens_above, dens_send.at[1], dens_recv.at[1], l, v + 1)

    def edge_up(c):
        return copy(
            edge_top.at[c], below.at[c], edge_send.at[0, c], edge_recv.at[0, c], l + 1, v - 1
        )

    def edge_down(c):
        return copy(
            edge_bottom.at[c], above.at[c], edge_send.at[1, c], edge_recv.at[1, c], l + 1, v + 1
        )

    def wide_up(c):
        return copy(
            wide_top.at[c], seed_below.at[c], wide_send.at[0, c], wide_recv.at[0, c], l + 2, v - 1
        )

    def wide_down(c):
        return copy(
            wide_bottom.at[c], seed_above.at[c], wide_send.at[1, c], wide_recv.at[1, c], l + 2, v + 1
        )

    def own_on(c, dl):
        return copy(passed.at[c], own.at[c], own_send.at[dl - 1, c], own_recv.at[c], l + dl, v)

    def swap(send, got, sems, recvs, step):
        target = lax.rem(v + step, views)
        return copy(send.at[target], got.at[v], sems.at[step], recvs.at[step], l, target)

    def seed_up(c):
        return copy(
            seed_top.at[c], seed_below.at[c], seed_send.at[0, c], seed_recv.at[0, c], l, v - 1
        )

    def seed_down(c):
        return copy(
            seed_bottom.at[c], seed_above.at[c], seed_send.at[1, c], seed_recv.at[1, c], l, v + 1
        )

    def first_up(s):
        return copy(
            first_top.at[s], first_below.at[s], first_send.at[0, s], first_recv.at[0, s], l + 1, v - 1
        )

    def first_down(s):
        return copy(
            first_bottom.at[s], first_above.at[s], first_send.at[1, s], first_recv.at[1, s], l + 1, v + 1
        )

    def first_on(s):
        return copy(
            density_hbm.at[s], first.at[s], first_send.at[2, s], first_recv.at[2, s], l + 1, v
        )

    @pl.when(has_above)
    def _():
        dens_up().start()

    @pl.when(has_below)
    def _():
        dens_down().start()

    for c in range(channels):

        @pl.when((l <= 1) & has_above)
        def _():
            seed_up(c).start()

        @pl.when((l <= 1) & has_below)
        def _():
            seed_down(c).start()

    for s in range(slices):

        @pl.when(gives & has_above)
        def _():
            first_up(s).start()

        @pl.when(gives & has_below)
        def _():
            first_down(s).start()

        @pl.when(gives)
        def _():
            first_on(s).start()

    row = lax.broadcasted_iota(jnp.int32, (height, width), 0)
    for s in range(slices):
        opacity = opacity_of(density_ref[s])
        ring_opacity[s, :height, :] = opacity
        alpha = view_scale * opacity
        run = 1.0 - alpha
        reach = 1
        while reach < height:
            run = run * jnp.where(row >= reach, pltpu.roll(run, reach, 0), 1.0)
            reach *= 2
        before = jnp.where(row >= 1, pltpu.roll(run, 1, 0), 1.0)
        weight[0, s] = before * alpha
        last = run[height - 1 :, :]
        for c in range(channels + 1):
            place = c * slices + s
            rows_b[place : place + 1, :] = last
        place = channels * slices + s
        rows_a[place : place + 1, :] = 1.0 - last
    for block in range(views):
        send_b[block] = rows_b[:, block * cols : (block + 1) * cols]

    for step in range(1, views):
        swap(send_b, got_b, b_send, b_recv, step).start()
    loads[2].wait()

    for s in range(slices):
        base = weight[0, s]
        for c in reversed(range(channels)):
            weight[c, s] = base * colour_ref[c, s].astype(jnp.float32)

    @pl.when(has_above)
    def _():
        dens_down().wait_recv()

    @pl.when(has_below)
    def _():
        dens_up().wait_recv()

    for s in range(slices):
        ring_opacity[s, height:, :] = jnp.zeros((spare, width), jnp.float32)
        ring_opacity[s, height : height + slices, :] = opacity_of(dens_below[s])
        ring_opacity[s, height + spare - slices :, :] = opacity_of(dens_above[s])
    plane_ref[height:, :] = jnp.zeros((spare, width), jnp.float32)

    ring_row = lax.broadcasted_iota(jnp.int32, (height + spare, width), 0)
    column = lax.broadcasted_iota(jnp.int32, (height + spare, width), 1)
    not_left = column > 0
    not_right = column < width - 1
    low = jnp.where(has_below, height + spare // 2, height)
    high = jnp.where(has_above, height + spare // 2, height + spare)
    inside = (ring_row < low) | (ring_row >= high)

    def blur(p):
        across = jnp.where(not_left, pltpu.roll(p, 1, 1), 0.0) + jnp.where(
            not_right, pltpu.roll(p, width - 1, 1), 0.0
        )
        middle = blur_center * p + blur_edge * across
        side = blur_edge * p + blur_corner * across
        total = height + spare
        return middle + (pltpu.roll(side, 1, 0) + pltpu.roll(side, total - 1, 0))

    for s in range(slices):

        @pl.when(takes & has_above)
        def _():
            first_down(s).wait_recv()

        @pl.when(takes & has_below)
        def _():
            first_up(s).wait_recv()

        @pl.when(takes)
        def _():
            first_on(s).wait_recv()
            first_opacity[s, :height, :] = opacity_of(first[s])
            first_opacity[s, height:, :] = jnp.zeros((spare, width), jnp.float32)
            first_opacity[s, height : height + reach2, :] = opacity_of(first_below[s])
            first_opacity[s, height + spare - reach2 :, :] = opacity_of(first_above[s])

    for c in range(channels):
        decay = absorb_ref[c]

        @pl.when((l <= 1) & has_above)
        def _():
            seed_down(c).wait_recv()

        @pl.when((l <= 1) & has_below)
        def _():
            seed_up(c).wait_recv()

        @pl.when(l > 1)
        def _():
            own_on(c, 1).wait_recv()

        @pl.when(even & (l > 1) & has_above)
        def _():
            wide_down(c).wait_recv()

        @pl.when(even & (l > 1) & has_below)
        def _():
            wide_up(c).wait_recv()

        @pl.when(odd & (l > 1) & has_above)
        def _():
            edge_down(c).wait_recv()

        @pl.when(odd & (l > 1) & has_below)
        def _():
            edge_up(c).wait_recv()

        @pl.when(l <= 1)
        def _():
            plane_ref[:height, :] = light_ref[c]

        @pl.when(l > 1)
        def _():
            plane_ref[:height, :] = own[c]

        @pl.when(even | (l == 1))
        def _():
            plane_ref[height : height + reach2, :] = seed_below[c]
            plane_ref[height + spare - reach2 :, :] = seed_above[c]

        @pl.when(odd & (l > 1))
        def _():
            plane_ref[height : height + slices, :] = below[c]
            plane_ref[height + spare - slices :, :] = above[c]

        @pl.when(takes)
        def _():
            swept = plane_ref[...]
            for s in range(slices):
                swept = blur(swept * (1.0 - decay * first_opacity[s]))
                swept = jnp.where(inside, swept, 0.0)
            plane_ref[...] = swept

        plane = plane_ref[...]
        for s in range(slices):
            lit = jnp.sum(weight[c, s] * plane[:height], axis=0, keepdims=True)
            place = c * slices + s
            rows_a[place : place + 1, :] = lit
            dimmed = plane * (1.0 - decay * ring_opacity[s])
            if s < slices - 1:
                plane = jnp.where(inside, blur(dimmed), 0.0)

        @pl.when(jumps | steps)
        def _():
            after = blur(dimmed)
            passed[c] = after[:height]
            edge_top[c] = after[:slices]
            edge_bottom[c] = after[height - slices : height]
            wide_top[c] = after[:reach2]
            wide_bottom[c] = after[height - reach2 : height]

        @pl.when(jumps & has_above)
        def _():
            wide_up(c).start()

        @pl.when(jumps & has_below)
        def _():
            wide_down(c).start()

        @pl.when(jumps)
        def _():
            own_on(c, 2).start()

        @pl.when(steps & has_above)
        def _():
            edge_up(c).start()

        @pl.when(steps & has_below)
        def _():
            edge_down(c).start()

        @pl.when(steps)
        def _():
            own_on(c, 1).start()

    for block in range(views):
        send_a[block] = rows_a[:, block * cols : (block + 1) * cols]
    for step in range(1, views):
        swap(send_a, got_a, a_send, a_recv, step).start()
    got_a[v] = send_a[v]
    got_b[v] = send_b[v]
    for step in range(1, views):
        swap(send_b, got_b, b_send, b_recv, step).wait_recv()
    for step in range(1, views):
        swap(send_a, got_a, a_send, a_recv, step).wait_recv()
    image = got_a[0]
    shade = got_b[0]
    for front in range(1, views):
        image = image + shade * got_a[front]
        if front < views - 1:
            shade = shade * got_b[front]
    out_ref[...] = image

    for step in range(1, views):
        swap(send_b, got_b, b_send, b_recv, step).wait_send()
        swap(send_a, got_a, a_send, a_recv, step).wait_send()

    @pl.when(has_above)
    def _():
        dens_up().wait_send()

    @pl.when(has_below)
    def _():
        dens_down().wait_send()

    for c in range(channels):

        @pl.when(jumps & has_above)
        def _():
            wide_up(c).wait_send()

        @pl.when(jumps & has_below)
        def _():
            wide_down(c).wait_send()

        @pl.when(jumps)
        def _():
            own_on(c, 2).wait_send()

        @pl.when(steps & has_above)
        def _():
            edge_up(c).wait_send()

        @pl.when(steps & has_below)
        def _():
            edge_down(c).wait_send()

        @pl.when(steps)
        def _():
            own_on(c, 1).wait_send()

    for c in range(channels):

        @pl.when((l <= 1) & has_above)
        def _():
            seed_up(c).wait_send()

        @pl.when((l <= 1) & has_below)
        def _():
            seed_down(c).wait_send()

    for s in range(slices):

        @pl.when(gives & has_above)
        def _():
            first_up(s).wait_send()

        @pl.when(gives & has_below)
        def _():
            first_down(s).wait_send()

        @pl.when(gives)
        def _():
            first_on(s).wait_send()


def column_kernel(
    lights,
    views,
    halo,
    density_hbm,
    colour_hbm,
    absorb_ref,
    light_hbm,
    out_ref,
    dens_rows,
    light_rows,
    colour_rows,
    colour_wide,
    dens_ring,
    light_ring,
    dens_in,
    light_in,
    colour_in,
    first_in,
    dens_op,
    first_op,
    inside_ref,
    planes,
    lit,
    weight,
    chain_in,
    chain_out,
    load_sem,
    dens_send,
    dens_recv,
    ring_send,
    ring_recv,
    light_send,
    light_recv,
    seam_send,
    seam_recv,
    colour_send,
    colour_recv,
    first_send,
    first_recv,
    chain_send,
    chain_recv,
):
    l = lax.axis_index("light")
    v = lax.axis_index("view")
    slices, height, width = dens_rows.shape
    channels = light_rows.shape[0]
    cols = width // views
    tall = views * height
    wide = cols + 2 * halo
    f32 = jnp.float32
    has_next = l < lights - 1

    barrier = pltpu.get_barrier_semaphore()

    def greet(to_l, to_v):
        pl.semaphore_signal(
            barrier, inc=1, device_id={"light": to_l, "view": to_v}, device_id_type=MESH
        )

    for step in range(1, views):
        greet(l, lax.rem(v + step, views))

    @pl.when(l == 1)
    def _():
        for step in range(views):
            greet(l - 1, lax.rem(v + step, views))

    @pl.when(l > 1)
    def _():
        greet(l - 1, v)

    loads = [
        pltpu.make_async_copy(src, dst, load_sem.at[i])
        for i, (src, dst) in enumerate(
            ((density_hbm, dens_rows), (light_hbm, light_rows), (colour_hbm, colour_rows))
        )
    ]
    for load in loads:
        load.start()

    def block(b):
        return slice(b * cols, (b + 1) * cols)

    lane = lax.broadcasted_iota(jnp.int32, (height, cols), 1)

    def build_ring(ring, rows):
        for b in range(views):
            tile = jnp.zeros((height, cols), f32)
            for k in range(rows.shape[0]):
                start = 2 * halo * k
                right = rows[k, :, block((b + 1) % views)]
                left = rows[k, :, block((b - 1) % views)]
                if start:
                    right = pltpu.roll(right, start, 1)
                    left = pltpu.roll(left, start, 1)
                low = (start - halo) % cols
                tile = jnp.where((lane >= start) & (lane < start + halo), right, tile)
                tile = jnp.where((lane >= low) & (lane < low + halo), left, tile)
            ring[b] = tile

    loads[0].wait()
    build_ring(dens_ring, dens_rows)
    loads[1].wait()

    @pl.when(l <= 1)
    def _():
        build_ring(light_ring, light_rows)

    zero = jnp.int32(0)
    others = jnp.where(l == 0, jnp.int32(views), jnp.where(has_next, jnp.int32(1), zero))
    pl.semaphore_wait(barrier, views - 1 + others)

    def aim(step):
        target = lax.rem(v + step, views)
        return target, pl.ds(pl.multiple_of(target * cols, cols), cols)

    here = pl.ds(pl.multiple_of(v * height, height), height)

    def copy(src, dst, send, recv, to_l, to_v):
        return pltpu.make_async_remote_copy(
            src_ref=src,
            dst_ref=dst,
            send_sem=send,
            recv_sem=recv,
            device_id={"light": to_l, "view": to_v},
            device_id_type=MESH,
        )

    def move(src, dst, sends, recvs, step, target):
        if step == 0:
            return pltpu.make_async_copy(src, dst, recvs.at[0])
        return copy(src, dst, sends.at[step], recvs.at[step], l, target)

    def dens_move(step):
        target, there = aim(step)
        return move(
            density_hbm.at[:, :, there], dens_in.at[:slices, here, :], dens_send, dens_recv, step, target
        )

    def ring_move(step):
        target, there = aim(step)
        return move(dens_ring.at[target], dens_in.at[slices, here, :], ring_send, ring_recv, step, target)

    def light_move(step):
        target, there = aim(step)
        return move(
            light_hbm.at[:, :, there], light_in.at[:channels, here, :], light_send, light_recv, step, target
        )

    def seam_move(step):
        target, there = aim(step)
        return move(light_ring.at[target], light_in.at[channels, here, :], seam_send, seam_recv, step, target)

    def colour_move(step):
        target, there = aim(step)
        return move(colour_wide.at[:, :, there], colour_in.at[:, here, :], colour_send, colour_recv, step, target)

    def first_move(s, step):
        target, there = aim(step)
        src = dens_ring.at[target] if s == slices else density_hbm.at[s, :, there]
        return copy(
            src, first_in.at[s, here, :], first_send.at[s, step], first_recv.at[s, step], l + 1, target
        )

    def chain_move(c):
        return copy(chain_out.at[c], chain_in.at[c], chain_send.at[c], chain_recv.at[c], l + 1, v)

    @pl.when(l == 0)
    def _():
        for s in (slices, *range(slices)):
            for step in range(views):
                first_move(s, step).start()

    @pl.when(l <= 1)
    def _():
        for step in range(views):
            seam_move(step).start()
            light_move(step).start()

    for step in range(views):
        ring_move(step).start()
        dens_move(step).start()

    loads[2].wait()
    for c in range(channels):
        for s in range(slices):
            colour_wide[c * slices + s] = colour_rows[c, s].astype(f32)
    for step in range(views):
        colour_move(step).start()

    def wait_all(move_of):
        for step in range(views):
            if step == 0:
                move_of(step).wait()
            else:
                move_of(step).wait_recv()

    def place(dst, plane, ring, k):
        start = 2 * halo * k
        low = (start - halo) % cols
        dst[:halo, :] = ring[low : low + halo]
        dst[halo : halo + cols, :] = plane
        dst[halo + cols :, :] = ring[start : start + halo]

    ring_row = lax.broadcasted_iota(jnp.int32, (wide, tall), 0)
    low = jnp.where(v > 0, 0, halo)
    high = jnp.where(v < views - 1, wide, wide - halo)
    inside_ref[...] = jnp.where((ring_row >= low) & (ring_row < high), 1.0, 0.0)

    ring_lane = lax.broadcasted_iota(jnp.int32, (wide, tall), 1)
    not_first = ring_lane > 0
    not_last = ring_lane < tall - 1

    def blur(p):
        across = jnp.where(not_first, pltpu.roll(p, 1, 1), 0.0) + jnp.where(
            not_last, pltpu.roll(p, tall - 1, 1), 0.0
        )
        middle = blur_center * p + blur_edge * across
        side = blur_edge * p + blur_corner * across
        return middle + (pltpu.roll(side, 1, 0) + pltpu.roll(side, wide - 1, 0))

    def opacities(dst, src, ring, s):
        place(dst.at[s], src[s].T, ring, s)
        dst[s] = inside_ref[...] * opacity_of(dst[s])

    def pass_slice(plane, opacity, decay):
        return blur(plane * (inside_ref[...] - decay * opacity))

    row8 = lax.broadcasted_iota(jnp.int32, (out_ref.shape[0], tall), 0)
    lane8 = lax.broadcasted_iota(jnp.int32, (out_ref.shape[0], tall), 1)

    def gather(items):
        picks = []
        parts = []
        for value, pick in items:
            large = value.astype(jnp.bfloat16)
            small = (value - large.astype(f32)).astype(jnp.bfloat16)
            pick = jnp.where(pick, 1.0, 0.0).astype(jnp.bfloat16)
            picks += [pick, pick]
            parts += [large, small]
        return lax.dot_general(
            jnp.concatenate(picks, axis=1),
            jnp.concatenate(parts, axis=1),
            (((1,), (1,)), ((), ())),
            preferred_element_type=f32,
        )

    def own_opacity():
        wait_all(ring_move)
        wait_all(dens_move)
        ring = dens_in[slices].T
        for s in range(slices):
            opacities(dens_op, dens_in, ring, s)

    def weights():
        y = lax.broadcasted_iota(jnp.int32, (cols, tall), 1)
        shade = []
        bases = []
        for s in range(slices):
            alpha = view_scale * dens_op[s, halo : halo + cols, :]
            run = 1.0 - alpha
            reach = 1
            while reach < tall:
                run = run * jnp.where(y >= reach, pltpu.roll(run, reach, 1), 1.0)
                reach *= 2
            before = jnp.where(y >= 1, pltpu.roll(run, 1, 1), 1.0)
            bases.append(before * alpha)
            shade.append((1.0 - run, (row8 == channels * slices + s) & (lane8 == tall - 1)))
        out_ref[...] = gather(shade)
        wait_all(colour_move)
        for s in range(slices):
            for c in range(channels):
                weight[c, s] = bases[s] * colour_in[c * slices + s].T

    def composite(c):
        out_ref[...] += gather(
            [(weight[c, s] * lit[c, s], row8 == c * slices + s) for s in range(slices)]
        )

    @pl.when(l <= 1)
    def _():
        wait_all(seam_move)
        wait_all(light_move)
        ring = light_in[channels].T
        for c in range(channels):
            place(planes.at[c], light_in[c].T, ring, c)

    @pl.when(l == 1)
    def _():
        for s in (slices, 0):
            for step in range(views):
                first_move(s, step).wait_recv()
        ring = first_in[slices].T
        for s in range(slices):
            if s > 0:
                for step in range(views):
                    first_move(s, step).wait_recv()
            opacities(first_op, first_in, ring, s)
            if s < slices - 1:
                for c in range(channels):
                    planes[c] = pass_slice(planes[c], first_op[s], absorb_ref[c])
        own_opacity()

    @pl.when(l != 1)
    def _():
        own_opacity()
        weights()

    for c in range(channels):
        decay = absorb_ref[c]

        @pl.when(l == 1)
        def _():
            planes[c] = pass_slice(planes[c], first_op[slices - 1], decay)

        @pl.when(l > 1)
        def _():
            chain_move(c).wait_recv()
            planes[c] = chain_in[c]

        plane = planes[c]
        for s in range(slices):
            lit[c, s] = plane[halo : halo + cols, :]
            if s < slices - 1:
                plane = pass_slice(plane, dens_op[s], decay)

        @pl.when((l >= 1) & has_next)
        def _():
            chain_out[c] = pass_slice(plane, dens_op[slices - 1], decay)
            chain_move(c).start()

        @pl.when(l != 1)
        def _():
            composite(c)

    @pl.when(l == 1)
    def _():
        weights()
        for c in range(channels):
            composite(c)

    for step in range(1, views):
        dens_move(step).wait_send()
        ring_move(step).wait_send()
        colour_move(step).wait_send()

    @pl.when(l <= 1)
    def _():
        for step in range(1, views):
            light_move(step).wait_send()
            seam_move(step).wait_send()

    @pl.when(l == 0)
    def _():
        for s in range(slices + 1):
            for step in range(views):
                first_move(s, step).wait_send()

    @pl.when((l >= 1) & has_next)
    def _():
        for c in range(channels):
            chain_move(c).wait_send()


def by_columns(lights, views, halo, density, colour, absorb, light_in):
    slices, height, width = density.shape
    channels = light_in.shape[0]
    cols = width // views
    tall = views * height
    wide = cols + 2 * halo
    rows = (channels + 1) * slices
    f32 = jnp.float32
    dma = pltpu.SemaphoreType.DMA
    hbm = pl.BlockSpec(memory_space=pl.ANY)
    ring = pltpu.VMEM((views, height, cols), f32)
    spread = pltpu.VMEM((slices + 1, tall, cols), f32)
    opacity = pltpu.VMEM((slices, wide, tall), f32)
    lights3 = pltpu.VMEM((channels, wide, tall), f32)
    voxels = pltpu.VMEM((channels, slices, cols, tall), f32)
    image = pl.pallas_call(
        functools.partial(column_kernel, lights, views, halo),
        out_shape=pltpu.VMEM((rows, cols), f32),
        in_specs=[hbm, hbm, pl.BlockSpec(memory_space=pltpu.SMEM), hbm],
        out_specs=pl.BlockSpec(memory_space=pltpu.VMEM),
        scratch_shapes=[
            pltpu.VMEM(density.shape, density.dtype),
            pltpu.VMEM(light_in.shape, light_in.dtype),
            pltpu.VMEM(colour.shape, colour.dtype),
            pltpu.VMEM((channels * slices, height, width), f32),
            ring,
            ring,
            spread,
            pltpu.VMEM((channels + 1, tall, cols), f32),
            pltpu.VMEM((channels * slices, tall, cols), f32),
            spread,
            opacity,
            opacity,
            pltpu.VMEM((wide, tall), f32),
            lights3,
            voxels,
            voxels,
            lights3,
            lights3,
            dma((3,)),
            *[dma((views,))] * 10,
            dma((slices + 1, views)),
            dma((slices + 1, views)),
            dma((channels,)),
            dma((channels,)),
        ],
        compiler_params=pltpu.CompilerParams(collective_id=0, has_side_effects=True),
    )(density, colour, absorb, light_in)
    return image.reshape(channels + 1, slices, cols)


def on_device(lights, views, density, colour, absorb, light_in):
    slices, height, width = density.shape
    channels = light_in.shape[0]
    cols = width // views
    halo = -(-(lights * slices - 1) // 8) * 8
    whole_tiles = cols % 128 == 0 and views * height == 128 and height % 8 == 0
    packs = 2 * halo * max(channels, slices) <= cols
    if lights > 1 and whole_tiles and packs:
        return by_columns(lights, views, halo, density, colour, absorb, light_in)
    rows = (channels + 1) * slices
    spare = -(-4 * slices // 8) * 8
    reach2 = 2 * slices
    f32 = jnp.float32
    edges = pltpu.VMEM((channels, slices, width), f32)
    dens_edges = pltpu.VMEM((slices, slices, width), f32)
    plane = pltpu.VMEM((channels, height, width), f32)
    blocks = pltpu.VMEM((views, rows, cols), f32)
    dma = pltpu.SemaphoreType.DMA
    vmem = pl.BlockSpec(memory_space=pltpu.VMEM)
    hbm = pl.BlockSpec(memory_space=pl.ANY)
    first_edges = pltpu.VMEM((slices, reach2, width), f32)
    seeds = pltpu.VMEM((channels, reach2, width), f32)
    ring_slices = pltpu.VMEM((slices, height + spare, width), f32)
    image = pl.pallas_call(
        functools.partial(kernel, lights, views),
        out_shape=pltpu.VMEM((rows, cols), f32),
        in_specs=[hbm, hbm, pl.BlockSpec(memory_space=pltpu.SMEM), hbm],
        out_specs=vmem,
        scratch_shapes=[
            pltpu.VMEM(density.shape, density.dtype),
            pltpu.VMEM(colour.shape, colour.dtype),
            plane,
            dma((3,)),
            pltpu.VMEM(density.shape, density.dtype),
            first_edges,
            first_edges,
            first_edges,
            first_edges,
            ring_slices,
            dma((3, slices)),
            dma((3, slices)),
            seeds,
            seeds,
            dma((2, channels)),
            pltpu.VMEM((height + spare, width), f32),
            seeds,
            seeds,
            dma((2, channels)),
            dma((2, channels)),
            plane,
            edges,
            edges,
            plane,
            edges,
            edges,
            seeds,
            seeds,
            dens_edges,
            dens_edges,
            dens_edges,
            dens_edges,
            ring_slices,
            pltpu.VMEM((channels, slices, height, width), f32),
            pltpu.VMEM((rows, width), f32),
            pltpu.VMEM((rows, width), f32),
            blocks,
            blocks,
            blocks,
            blocks,
            dma((2, channels)),
            dma((channels,)),
            dma((2, channels)),
            dma((2, channels)),
            dma((2, channels)),
            dma((2,)),
            dma((2,)),
            dma((views,)),
            dma((views,)),
            dma((views,)),
            dma((views,)),
        ],
        compiler_params=pltpu.CompilerParams(collective_id=0, has_side_effects=True),
    )(density, colour, absorb, light_in)
    return image.reshape(channels + 1, slices, cols)


def solution(mesh):
    return jax.shard_map(
        functools.partial(on_device, mesh.shape["light"], mesh.shape["view"]),
        mesh=mesh,
        in_specs=(
            P("light", "view", None),
            P(None, "light", "view", None),
            P(),
            P(None, "view", None),
        ),
        out_specs=P(None, "light", "view"),
        check_vma=False,
    )
```

```python
import functools

import jax
import jax.numpy as jnp
from jax import lax
from jax.experimental import pallas as pl
from jax.experimental.pallas import tpu as pltpu
from jax.sharding import PartitionSpec as P

view_scale = 0.25
blur_center = 0.5
blur_edge = 0.1
blur_corner = 0.025

MESH = pl.DeviceIdType.MESH


def opacity_of(values):
    return 0.01 * values + 0.03 * values * values * values


def kernel(
    lights,
    views,
    density_hbm,
    colour_hbm,
    absorb_ref,
    light_hbm,
    out_ref,
    density_ref,
    colour_ref,
    light_ref,
    load_sem,
    first,
    first_top,
    first_bottom,
    first_above,
    first_below,
    first_opacity,
    first_send,
    first_recv,
    seed_above,
    seed_below,
    seed_recv,
    plane_ref,
    wide_top,
    wide_bottom,
    wide_send,
    wide_recv,
    own,
    above,
    below,
    passed,
    edge_top,
    edge_bottom,
    seed_top,
    seed_bottom,
    dens_top,
    dens_bottom,
    dens_above,
    dens_below,
    ring_opacity,
    weight,
    rows_a,
    rows_b,
    send_a,
    send_b,
    got_a,
    got_b,
    own_send,
    own_recv,
    edge_send,
    edge_recv,
    seed_send,
    dens_send,
    dens_recv,
    a_send,
    a_recv,
    b_send,
    b_recv,
):
    l = lax.axis_index("light")
    v = lax.axis_index("view")
    slices, height, width = density_ref.shape
    channels = light_ref.shape[0]
    spare = plane_ref.shape[0] - height
    reach2 = seed_above.shape[1]
    cols = out_ref.shape[1]
    has_above = v > 0
    has_below = v < views - 1
    has_next = l < lights - 1
    is_first = l == 0
    even = lax.rem(l, 2) == 0
    odd = lax.rem(l, 2) == 1
    gives = (is_first | odd) & has_next
    takes = (l == 1) | (even & (l > 1))
    jumps = even & (l < lights - 2)
    steps = even & (l > 1) & has_next

    barrier = pltpu.get_barrier_semaphore()

    def greet(dl, dv):
        pl.semaphore_signal(
            barrier, inc=1, device_id={"light": l + dl, "view": v + dv}, device_id_type=MESH
        )

    for step in range(1, views):
        pl.semaphore_signal(
            barrier,
            inc=1,
            device_id={"light": l, "view": lax.rem(v + step, views)},
            device_id_type=MESH,
        )
    for dl in (-2, -1, 1, 2):
        l_ok = l >= -dl if dl < 0 else l < lights - dl
        if abs(dl) == 2:
            l_ok = l_ok & even

        @pl.when(l_ok)
        def _():
            greet(dl, 0)

        for dv in (-1, 1):

            @pl.when(l_ok & (has_above if dv < 0 else has_below))
            def _():
                greet(dl, dv)

    one = jnp.int32(1)
    zero = jnp.int32(0)
    lines = jnp.where(l > 0, one, zero) + jnp.where(has_next, one, zero)
    lines = lines + jnp.where(even & (l > 1), one, zero) + jnp.where(jumps, one, zero)
    sides = one + jnp.where(has_above, one, zero) + jnp.where(has_below, one, zero)

    loads = [
        pltpu.make_async_copy(src, dst, load_sem.at[i])
        for i, (src, dst) in enumerate(
            ((density_hbm, density_ref), (light_hbm, light_ref), (colour_hbm, colour_ref))
        )
    ]
    for load in loads:
        load.start()

    @pl.when(jnp.logical_not(has_above))
    def _():
        above[...] = jnp.zeros_like(above)
        dens_above[...] = jnp.zeros_like(dens_above)
        first_above[...] = jnp.zeros_like(first_above)
        seed_above[...] = jnp.zeros_like(seed_above)

    @pl.when(jnp.logical_not(has_below))
    def _():
        below[...] = jnp.zeros_like(below)
        dens_below[...] = jnp.zeros_like(dens_below)
        first_below[...] = jnp.zeros_like(first_below)
        seed_below[...] = jnp.zeros_like(seed_below)

    loads[0].wait()
    dens_top[...] = density_ref[:, :slices, :]
    dens_bottom[...] = density_ref[:, height - slices :, :]

    @pl.when(gives)
    def _():
        first_top[...] = density_ref[:, :reach2, :]
        first_bottom[...] = density_ref[:, height - reach2 :, :]

    loads[1].wait()

    @pl.when(l <= 1)
    def _():
        seed_top[...] = light_ref[:, :reach2, :]
        seed_bottom[...] = light_ref[:, height - reach2 :, :]

    pl.semaphore_wait(barrier, views - 1 + lines * sides)

    def copy(src, dst, send, recv, to_l, to_v):
        return pltpu.make_async_remote_copy(
            src_ref=src,
            dst_ref=dst,
            send_sem=send,
            recv_sem=recv,
            device_id={"light": to_l, "view": to_v},
            device_id_type=MESH,
        )

    def dens_up():
        return copy(dens_top, dens_below, dens_send.at[0], dens_recv.at[0], l, v - 1)

    def dens_down():
        return copy(dens_bottom, dens_above, dens_send.at[1], dens_recv.at[1], l, v + 1)

    def edge_up(c):
        return copy(
            edge_top.at[c], below.at[c], edge_send.at[0, c], edge_recv.at[0, c], l + 1, v - 1
        )

    def edge_down(c):
        return copy(
            edge_bottom.at[c], above.at[c], edge_send.at[1, c], edge_recv.at[1, c], l + 1, v + 1
        )

    def wide_up(c):
        return copy(
            wide_top.at[c], seed_below.at[c], wide_send.at[0, c], wide_recv.at[0, c], l + 2, v - 1
        )

    def wide_down(c):
        return copy(
            wide_bottom.at[c], seed_above.at[c], wide_send.at[1, c], wide_recv.at[1, c], l + 2, v + 1
        )

    def own_on(c, dl):
        return copy(passed.at[c], own.at[c], own_send.at[dl - 1, c], own_recv.at[c], l + dl, v)

    def swap(send, got, sems, recvs, step):
        target = lax.rem(v + step, views)
        return copy(send.at[target], got.at[v], sems.at[step], recvs.at[step], l, target)

    def seed_up(c):
        return copy(
            seed_top.at[c], seed_below.at[c], seed_send.at[0, c], seed_recv.at[0, c], l, v - 1
        )

    def seed_down(c):
        return copy(
            seed_bottom.at[c], seed_above.at[c], seed_send.at[1, c], seed_recv.at[1, c], l, v + 1
        )

    def first_up(s):
        return copy(
            first_top.at[s], first_below.at[s], first_send.at[0, s], first_recv.at[0, s], l + 1, v - 1
        )

    def first_down(s):
        return copy(
            first_bottom.at[s], first_above.at[s], first_send.at[1, s], first_recv.at[1, s], l + 1, v + 1
        )

    def first_on(s):
        return copy(
            density_hbm.at[s], first.at[s], first_send.at[2, s], first_recv.at[2, s], l + 1, v
        )

    @pl.when(has_above)
    def _():
        dens_up().start()

    @pl.when(has_below)
    def _():
        dens_down().start()

    for c in range(channels):

        @pl.when((l <= 1) & has_above)
        def _():
            seed_up(c).start()

        @pl.when((l <= 1) & has_below)
        def _():
            seed_down(c).start()

    for s in range(slices):

        @pl.when(gives & has_above)
        def _():
            first_up(s).start()

        @pl.when(gives & has_below)
        def _():
            first_down(s).start()

        @pl.when(gives)
        def _():
            first_on(s).start()

    row = lax.broadcasted_iota(jnp.int32, (height, width), 0)
    for s in range(slices):
        opacity = opacity_of(density_ref[s])
        ring_opacity[s, :height, :] = opacity
        alpha = view_scale * opacity
        run = 1.0 - alpha
        reach = 1
        while reach < height:
            run = run * jnp.where(row >= reach, pltpu.roll(run, reach, 0), 1.0)
            reach *= 2
        before = jnp.where(row >= 1, pltpu.roll(run, 1, 0), 1.0)
        weight[0, s] = before * alpha
        last = run[height - 1 :, :]
        for c in range(channels + 1):
            place = c * slices + s
            rows_b[place : place + 1, :] = last
        place = channels * slices + s
        rows_a[place : place + 1, :] = 1.0 - last
    for block in range(views):
        send_b[block] = rows_b[:, block * cols : (block + 1) * cols]

    for step in range(1, views):
        swap(send_b, got_b, b_send, b_recv, step).start()
    loads[2].wait()

    for s in range(slices):
        base = weight[0, s]
        for c in reversed(range(channels)):
            weight[c, s] = base * colour_ref[c, s].astype(jnp.float32)

    @pl.when(has_above)
    def _():
        dens_down().wait_recv()

    @pl.when(has_below)
    def _():
        dens_up().wait_recv()

    for s in range(slices):
        ring_opacity[s, height:, :] = jnp.zeros((spare, width), jnp.float32)
        ring_opacity[s, height : height + slices, :] = opacity_of(dens_below[s])
        ring_opacity[s, height + spare - slices :, :] = opacity_of(dens_above[s])
    plane_ref[height:, :] = jnp.zeros((spare, width), jnp.float32)

    ring_row = lax.broadcasted_iota(jnp.int32, (height + spare, width), 0)
    column = lax.broadcasted_iota(jnp.int32, (height + spare, width), 1)
    not_left = column > 0
    not_right = column < width - 1
    low = jnp.where(has_below, height + spare // 2, height)
    high = jnp.where(has_above, height + spare // 2, height + spare)
    inside = (ring_row < low) | (ring_row >= high)

    def blur(p):
        across = jnp.where(not_left, pltpu.roll(p, 1, 1), 0.0) + jnp.where(
            not_right, pltpu.roll(p, width - 1, 1), 0.0
        )
        middle = blur_center * p + blur_edge * across
        side = blur_edge * p + blur_corner * across
        total = height + spare
        return middle + (pltpu.roll(side, 1, 0) + pltpu.roll(side, total - 1, 0))

    for s in range(slices):

        @pl.when(takes & has_above)
        def _():
            first_down(s).wait_recv()

        @pl.when(takes & has_below)
        def _():
            first_up(s).wait_recv()

        @pl.when(takes)
        def _():
            first_on(s).wait_recv()
            first_opacity[s, :height, :] = opacity_of(first[s])
            first_opacity[s, height:, :] = jnp.zeros((spare, width), jnp.float32)
            first_opacity[s, height : height + reach2, :] = opacity_of(first_below[s])
            first_opacity[s, height + spare - reach2 :, :] = opacity_of(first_above[s])

    for c in range(channels):
        decay = absorb_ref[c]

        @pl.when((l <= 1) & has_above)
        def _():
            seed_down(c).wait_recv()

        @pl.when((l <= 1) & has_below)
        def _():
            seed_up(c).wait_recv()

        @pl.when(l > 1)
        def _():
            own_on(c, 1).wait_recv()

        @pl.when(even & (l > 1) & has_above)
        def _():
            wide_down(c).wait_recv()

        @pl.when(even & (l > 1) & has_below)
        def _():
            wide_up(c).wait_recv()

        @pl.when(odd & (l > 1) & has_above)
        def _():
            edge_down(c).wait_recv()

        @pl.when(odd & (l > 1) & has_below)
        def _():
            edge_up(c).wait_recv()

        @pl.when(l <= 1)
        def _():
            plane_ref[:height, :] = light_ref[c]

        @pl.when(l > 1)
        def _():
            plane_ref[:height, :] = own[c]

        @pl.when(even | (l == 1))
        def _():
            plane_ref[height : height + reach2, :] = seed_below[c]
            plane_ref[height + spare - reach2 :, :] = seed_above[c]

        @pl.when(odd & (l > 1))
        def _():
            plane_ref[height : height + slices, :] = below[c]
            plane_ref[height + spare - slices :, :] = above[c]

        @pl.when(takes)
        def _():
            swept = plane_ref[...]
            for s in range(slices):
                swept = blur(swept * (1.0 - decay * first_opacity[s]))
                swept = jnp.where(inside, swept, 0.0)
            plane_ref[...] = swept

        plane = plane_ref[...]
        for s in range(slices):
            lit = jnp.sum(weight[c, s] * plane[:height], axis=0, keepdims=True)
            place = c * slices + s
            rows_a[place : place + 1, :] = lit
            dimmed = plane * (1.0 - decay * ring_opacity[s])
            if s < slices - 1:
                plane = jnp.where(inside, blur(dimmed), 0.0)

        @pl.when(jumps | steps)
        def _():
            after = blur(dimmed)
            passed[c] = after[:height]
            edge_top[c] = after[:slices]
            edge_bottom[c] = after[height - slices : height]
            wide_top[c] = after[:reach2]
            wide_bottom[c] = after[height - reach2 : height]

        @pl.when(jumps & has_above)
        def _():
            wide_up(c).start()

        @pl.when(jumps & has_below)
        def _():
            wide_down(c).start()

        @pl.when(jumps)
        def _():
            own_on(c, 2).start()

        @pl.when(steps & has_above)
        def _():
            edge_up(c).start()

        @pl.when(steps & has_below)
        def _():
            edge_down(c).start()

        @pl.when(steps)
        def _():
            own_on(c, 1).start()

    for block in range(views):
        send_a[block] = rows_a[:, block * cols : (block + 1) * cols]
    for step in range(1, views):
        swap(send_a, got_a, a_send, a_recv, step).start()
    got_a[v] = send_a[v]
    got_b[v] = send_b[v]
    for step in range(1, views):
        swap(send_b, got_b, b_send, b_recv, step).wait_recv()
    for step in range(1, views):
        swap(send_a, got_a, a_send, a_recv, step).wait_recv()
    image = got_a[0]
    shade = got_b[0]
    for front in range(1, views):
        image = image + shade * got_a[front]
        if front < views - 1:
            shade = shade * got_b[front]
    out_ref[...] = image

    for step in range(1, views):
        swap(send_b, got_b, b_send, b_recv, step).wait_send()
        swap(send_a, got_a, a_send, a_recv, step).wait_send()

    @pl.when(has_above)
    def _():
        dens_up().wait_send()

    @pl.when(has_below)
    def _():
        dens_down().wait_send()

    for c in range(channels):

        @pl.when(jumps & has_above)
        def _():
            wide_up(c).wait_send()

        @pl.when(jumps & has_below)
        def _():
            wide_down(c).wait_send()

        @pl.when(jumps)
        def _():
            own_on(c, 2).wait_send()

        @pl.when(steps & has_above)
        def _():
            edge_up(c).wait_send()

        @pl.when(steps & has_below)
        def _():
            edge_down(c).wait_send()

        @pl.when(steps)
        def _():
            own_on(c, 1).wait_send()

    for c in range(channels):

        @pl.when((l <= 1) & has_above)
        def _():
            seed_up(c).wait_send()

        @pl.when((l <= 1) & has_below)
        def _():
            seed_down(c).wait_send()

    for s in range(slices):

        @pl.when(gives & has_above)
        def _():
            first_up(s).wait_send()

        @pl.when(gives & has_below)
        def _():
            first_down(s).wait_send()

        @pl.when(gives)
        def _():
            first_on(s).wait_send()


def column_kernel(
    lights,
    views,
    halo,
    density_hbm,
    colour_hbm,
    absorb_ref,
    light_hbm,
    out_ref,
    dens_rows,
    light_rows,
    colour_rows,
    colour_wide,
    dens_ring,
    light_ring,
    dens_in,
    light_in,
    colour_in,
    dens_op,
    first_op,
    inside_ref,
    planes,
    lit,
    weight,
    chain_in,
    chain_out,
    load_sem,
    dens_send,
    dens_recv,
    ring_send,
    ring_recv,
    light_send,
    light_recv,
    seam_send,
    seam_recv,
    colour_send,
    colour_recv,
    first_send,
    first_recv,
    chain_send,
    chain_recv,
):
    l = lax.axis_index("light")
    v = lax.axis_index("view")
    slices, height, width = dens_rows.shape
    channels = light_rows.shape[0]
    cols = width // views
    tall = views * height
    wide = cols + 2 * halo
    f32 = jnp.float32
    has_next = l < lights - 1

    barrier = pltpu.get_barrier_semaphore()

    def greet(to_l, to_v):
        pl.semaphore_signal(
            barrier, inc=1, device_id={"light": to_l, "view": to_v}, device_id_type=MESH
        )

    for step in range(1, views):
        greet(l, lax.rem(v + step, views))

    @pl.when(l > 0)
    def _():
        greet(l - 1, v)

    loads = [
        pltpu.make_async_copy(src, dst, load_sem.at[i])
        for i, (src, dst) in enumerate(
            ((density_hbm, dens_rows), (light_hbm, light_rows), (colour_hbm, colour_rows))
        )
    ]
    for load in loads:
        load.start()

    def block(b):
        return slice(b * cols, (b + 1) * cols)

    lane = lax.broadcasted_iota(jnp.int32, (height, cols), 1)

    def build_ring(ring, rows):
        for b in range(views):
            tile = jnp.zeros((height, cols), f32)
            for k in range(rows.shape[0]):
                start = 2 * halo * k
                right = rows[k, :, block((b + 1) % views)]
                left = rows[k, :, block((b - 1) % views)]
                if start:
                    right = pltpu.roll(right, start, 1)
                    left = pltpu.roll(left, start, 1)
                low = (start - halo) % cols
                tile = jnp.where((lane >= start) & (lane < start + halo), right, tile)
                tile = jnp.where((lane >= low) & (lane < low + halo), left, tile)
            ring[b] = tile

    pl.semaphore_wait(barrier, views - 1 + jnp.where(has_next, jnp.int32(1), jnp.int32(0)))

    def aim(step):
        target = lax.rem(v + step, views)
        return target, pl.ds(pl.multiple_of(target * cols, cols), cols)

    here = pl.ds(pl.multiple_of(v * height, height), height)

    def copy(src, dst, send, recv, to_l, to_v):
        return pltpu.make_async_remote_copy(
            src_ref=src,
            dst_ref=dst,
            send_sem=send,
            recv_sem=recv,
            device_id={"light": to_l, "view": to_v},
            device_id_type=MESH,
        )

    def move(src, dst, sends, recvs, step, target):
        if step == 0:
            return pltpu.make_async_copy(src, dst, recvs.at[0])
        return copy(src, dst, sends.at[step], recvs.at[step], l, target)

    def dens_move(s, step):
        target, there = aim(step)
        return move(
            density_hbm.at[s, :, there], dens_in.at[s, here, :], dens_send.at[s], dens_recv.at[s], step, target
        )

    def ring_move(step):
        target, there = aim(step)
        return move(dens_ring.at[target], dens_in.at[slices, here, :], ring_send, ring_recv, step, target)

    def light_move(step):
        target, there = aim(step)
        return move(
            light_hbm.at[:, :, there], light_in.at[:channels, here, :], light_send, light_recv, step, target
        )

    def seam_move(step):
        target, there = aim(step)
        return move(light_ring.at[target], light_in.at[channels, here, :], seam_send, seam_recv, step, target)

    def colour_move(step):
        target, there = aim(step)
        return move(colour_wide.at[:, :, there], colour_in.at[:, here, :], colour_send, colour_recv, step, target)

    def first_move(s):
        return copy(dens_op.at[s], first_op.at[s], first_send.at[s], first_recv.at[s], l + 1, v)

    def chain_move(c):
        return copy(chain_out.at[c], chain_in.at[c], chain_send.at[c], chain_recv.at[c], l + 1, v)

    @pl.when(l == 1)
    def _():
        for step in range(views):
            light_move(step).start()

    for step in range(views):
        dens_move(0, step).start()

    loads[1].wait()

    @pl.when(l == 1)
    def _():
        build_ring(light_ring, light_rows)
        for step in range(views):
            seam_move(step).start()

    loads[0].wait()
    build_ring(dens_ring, dens_rows)
    for step in range(views):
        ring_move(step).start()
    for s in range(1, slices):
        for step in range(views):
            dens_move(s, step).start()

    @pl.when(l == 0)
    def _():
        for step in range(views):
            light_move(step).start()
        build_ring(light_ring, light_rows)
        for step in range(views):
            seam_move(step).start()

    loads[2].wait()
    for c in range(channels):
        for s in range(slices):
            colour_wide[c * slices + s] = colour_rows[c, s].astype(f32)
    for step in range(views):
        colour_move(step).start()

    def wait_all(move_of):
        for step in range(views):
            if step == 0:
                move_of(step).wait()
            else:
                move_of(step).wait_recv()

    def place(dst, plane, ring, k):
        start = 2 * halo * k
        low = (start - halo) % cols
        dst[:halo, :] = ring[low : low + halo]
        dst[halo : halo + cols, :] = plane
        dst[halo + cols :, :] = ring[start : start + halo]

    ring_row = lax.broadcasted_iota(jnp.int32, (wide, tall), 0)
    low = jnp.where(v > 0, 0, halo)
    high = jnp.where(v < views - 1, wide, wide - halo)
    inside_ref[...] = jnp.where((ring_row >= low) & (ring_row < high), 1.0, 0.0)

    ring_lane = lax.broadcasted_iota(jnp.int32, (wide, tall), 1)
    not_first = ring_lane > 0
    not_last = ring_lane < tall - 1

    def blur(p):
        across = jnp.where(not_first, pltpu.roll(p, 1, 1), 0.0) + jnp.where(
            not_last, pltpu.roll(p, tall - 1, 1), 0.0
        )
        middle = blur_center * p + blur_edge * across
        side = blur_edge * p + blur_corner * across
        return middle + (pltpu.roll(side, 1, 0) + pltpu.roll(side, wide - 1, 0))

    def opacities(dst, src, ring, s):
        place(dst.at[s], src[s].T, ring, s)
        dst[s] = inside_ref[...] * opacity_of(dst[s])

    def pass_slice(plane, opacity, decay):
        return blur(plane * (inside_ref[...] - decay * opacity))

    row8 = lax.broadcasted_iota(jnp.int32, (out_ref.shape[0], tall), 0)
    lane8 = lax.broadcasted_iota(jnp.int32, (out_ref.shape[0], tall), 1)

    def gather(items):
        picks = []
        parts = []
        for value, pick in items:
            large = value.astype(jnp.bfloat16)
            small = (value - large.astype(f32)).astype(jnp.bfloat16)
            pick = jnp.where(pick, 1.0, 0.0).astype(jnp.bfloat16)
            picks += [pick, pick]
            parts += [large, small]
        return lax.dot_general(
            jnp.concatenate(picks, axis=1),
            jnp.concatenate(parts, axis=1),
            (((1,), (1,)), ((), ())),
            preferred_element_type=f32,
        )

    def own_opacity():
        wait_all(ring_move)
        ring = dens_in[slices].T
        for s in range(slices):
            wait_all(functools.partial(dens_move, s))
            opacities(dens_op, dens_in, ring, s)

            @pl.when(l == 0)
            def _():
                first_move(s).start()

    def weights():
        y = lax.broadcasted_iota(jnp.int32, (cols, tall), 1)
        shade = []
        bases = []
        for s in range(slices):
            alpha = view_scale * dens_op[s, halo : halo + cols, :]
            run = 1.0 - alpha
            reach = 1
            while reach < tall:
                run = run * jnp.where(y >= reach, pltpu.roll(run, reach, 1), 1.0)
                reach *= 2
            before = jnp.where(y >= 1, pltpu.roll(run, 1, 1), 1.0)
            bases.append(before * alpha)
            shade.append((1.0 - run, (row8 == channels * slices + s) & (lane8 == tall - 1)))
        out_ref[...] = gather(shade)
        wait_all(colour_move)
        for s in range(slices):
            for c in range(channels):
                weight[c, s] = bases[s] * colour_in[c * slices + s].T

    def composite(c):
        out_ref[...] += gather(
            [(weight[c, s] * lit[c, s], row8 == c * slices + s) for s in range(slices)]
        )

    def gather_light():
        wait_all(seam_move)
        wait_all(light_move)
        ring = light_in[channels].T
        for c in range(channels):
            place(planes.at[c], light_in[c].T, ring, c)

    @pl.when(l == 1)
    def _():
        gather_light()
        for s in range(slices - 1):
            first_move(s).wait_recv()
            for c in range(channels):
                planes[c] = pass_slice(planes[c], first_op[s], absorb_ref[c])

    own_opacity()

    @pl.when(l == 1)
    def _():
        first_move(slices - 1).wait_recv()

    @pl.when(l != 1)
    def _():
        weights()

    @pl.when(l == 0)
    def _():
        gather_light()

    for c in range(channels):
        decay = absorb_ref[c]

        @pl.when(l == 1)
        def _():
            planes[c] = pass_slice(planes[c], first_op[slices - 1], decay)

        @pl.when(l > 1)
        def _():
            chain_move(c).wait_recv()
            planes[c] = chain_in[c]

        plane = planes[c]
        for s in range(slices):
            lit[c, s] = plane[halo : halo + cols, :]
            if s < slices - 1:
                plane = pass_slice(plane, dens_op[s], decay)

        @pl.when((l >= 1) & has_next)
        def _():
            chain_out[c] = pass_slice(plane, dens_op[slices - 1], decay)
            chain_move(c).start()

        @pl.when(l != 1)
        def _():
            composite(c)

    @pl.when(l == 1)
    def _():
        weights()
        for c in range(channels):
            composite(c)

    for step in range(1, views):
        for s in range(slices):
            dens_move(s, step).wait_send()
        ring_move(step).wait_send()
        colour_move(step).wait_send()

    @pl.when(l <= 1)
    def _():
        for step in range(1, views):
            light_move(step).wait_send()
            seam_move(step).wait_send()

    @pl.when(l == 0)
    def _():
        for s in range(slices):
            first_move(s).wait_send()

    @pl.when((l >= 1) & has_next)
    def _():
        for c in range(channels):
            chain_move(c).wait_send()


def by_columns(lights, views, halo, density, colour, absorb, light_in):
    slices, height, width = density.shape
    channels = light_in.shape[0]
    cols = width // views
    tall = views * height
    wide = cols + 2 * halo
    rows = (channels + 1) * slices
    f32 = jnp.float32
    dma = pltpu.SemaphoreType.DMA
    hbm = pl.BlockSpec(memory_space=pl.ANY)
    ring = pltpu.VMEM((views, height, cols), f32)
    spread = pltpu.VMEM((slices + 1, tall, cols), f32)
    opacity = pltpu.VMEM((slices, wide, tall), f32)
    lights3 = pltpu.VMEM((channels, wide, tall), f32)
    voxels = pltpu.VMEM((channels, slices, cols, tall), f32)
    image = pl.pallas_call(
        functools.partial(column_kernel, lights, views, halo),
        out_shape=pltpu.VMEM((rows, cols), f32),
        in_specs=[hbm, hbm, pl.BlockSpec(memory_space=pltpu.SMEM), hbm],
        out_specs=pl.BlockSpec(memory_space=pltpu.VMEM),
        scratch_shapes=[
            pltpu.VMEM(density.shape, density.dtype),
            pltpu.VMEM(light_in.shape, light_in.dtype),
            pltpu.VMEM(colour.shape, colour.dtype),
            pltpu.VMEM((channels * slices, height, width), f32),
            ring,
            ring,
            spread,
            pltpu.VMEM((channels + 1, tall, cols), f32),
            pltpu.VMEM((channels * slices, tall, cols), f32),
            opacity,
            opacity,
            pltpu.VMEM((wide, tall), f32),
            lights3,
            voxels,
            voxels,
            lights3,
            lights3,
            dma((3,)),
            dma((slices, views)),
            dma((slices, views)),
            *[dma((views,))] * 8,
            dma((slices,)),
            dma((slices,)),
            dma((channels,)),
            dma((channels,)),
        ],
        compiler_params=pltpu.CompilerParams(collective_id=0, has_side_effects=True),
    )(density, colour, absorb, light_in)
    return image.reshape(channels + 1, slices, cols)


def on_device(lights, views, density, colour, absorb, light_in):
    slices, height, width = density.shape
    channels = light_in.shape[0]
    cols = width // views
    halo = -(-(lights * slices - 1) // 8) * 8
    whole_tiles = cols % 128 == 0 and views * height == 128 and height % 8 == 0
    packs = 2 * halo * max(channels, slices) <= cols
    if lights > 1 and whole_tiles and packs:
        return by_columns(lights, views, halo, density, colour, absorb, light_in)
    rows = (channels + 1) * slices
    spare = -(-4 * slices // 8) * 8
    reach2 = 2 * slices
    f32 = jnp.float32
    edges = pltpu.VMEM((channels, slices, width), f32)
    dens_edges = pltpu.VMEM((slices, slices, width), f32)
    plane = pltpu.VMEM((channels, height, width), f32)
    blocks = pltpu.VMEM((views, rows, cols), f32)
    dma = pltpu.SemaphoreType.DMA
    vmem = pl.BlockSpec(memory_space=pltpu.VMEM)
    hbm = pl.BlockSpec(memory_space=pl.ANY)
    first_edges = pltpu.VMEM((slices, reach2, width), f32)
    seeds = pltpu.VMEM((channels, reach2, width), f32)
    ring_slices = pltpu.VMEM((slices, height + spare, width), f32)
    image = pl.pallas_call(
        functools.partial(kernel, lights, views),
        out_shape=pltpu.VMEM((rows, cols), f32),
        in_specs=[hbm, hbm, pl.BlockSpec(memory_space=pltpu.SMEM), hbm],
        out_specs=vmem,
        scratch_shapes=[
            pltpu.VMEM(density.shape, density.dtype),
            pltpu.VMEM(colour.shape, colour.dtype),
            plane,
            dma((3,)),
            pltpu.VMEM(density.shape, density.dtype),
            first_edges,
            first_edges,
            first_edges,
            first_edges,
            ring_slices,
            dma((3, slices)),
            dma((3, slices)),
            seeds,
            seeds,
            dma((2, channels)),
            pltpu.VMEM((height + spare, width), f32),
            seeds,
            seeds,
            dma((2, channels)),
            dma((2, channels)),
            plane,
            edges,
            edges,
            plane,
            edges,
            edges,
            seeds,
            seeds,
            dens_edges,
            dens_edges,
            dens_edges,
            dens_edges,
            ring_slices,
            pltpu.VMEM((channels, slices, height, width), f32),
            pltpu.VMEM((rows, width), f32),
            pltpu.VMEM((rows, width), f32),
            blocks,
            blocks,
            blocks,
            blocks,
            dma((2, channels)),
            dma((channels,)),
            dma((2, channels)),
            dma((2, channels)),
            dma((2, channels)),
            dma((2,)),
            dma((2,)),
            dma((views,)),
            dma((views,)),
            dma((views,)),
            dma((views,)),
        ],
        compiler_params=pltpu.CompilerParams(collective_id=0, has_side_effects=True),
    )(density, colour, absorb, light_in)
    return image.reshape(channels + 1, slices, cols)


def solution(mesh):
    return jax.shard_map(
        functools.partial(on_device, mesh.shape["light"], mesh.shape["view"]),
        mesh=mesh,
        in_specs=(
            P("light", "view", None),
            P(None, "light", "view", None),
            P(),
            P(None, "view", None),
        ),
        out_specs=P(None, "light", "view"),
        check_vma=False,
    )
```
